32 devices in a mesh: head: 2 (over core), ctx: 16 (over z, y, x).
Axes of the slice: x: 2, y: 2, z: 4, core: 2. Of those that a mesh axis runs over, the one named last changes fastest.
Arguments:
- queries: bfloat16 [4096, 4096], P(('ctx', 'head')), may hold values from -6 to 6
- keys: bfloat16 [4096, 512], P(('ctx', 'head')), may hold values from -6 to 6
- values: bfloat16 [4096, 512], P(('ctx', 'head')), may hold values from -6 to 6
- attn_out: bfloat16 [4096, 4096], P(('ctx', 'head')), may hold values from -6 to 6
- output_gradient: bfloat16 [4096, 4096], P(('ctx', 'head')), may hold values from -6 to 6
- doc_lengths: int32 [32], replicated, may hold values from 1 to 257, 4096 in all
Outputs:
- query_grad: bfloat16 [4096, 4096], P(('ctx', 'head'))
- key_gradient: bfloat16 [4096, 512], P(('ctx', 'head'))
- value_gradient: bfloat16 [4096, 512], P(('ctx', 'head'))
The draws below stay inside these ranges and needn't reach their ends.
Inputs may be any that keep to these rules, and one draw needn't show every extreme that they name: `doc_lengths`: documents fill the 4096 tokens in order; one document has exactly 257 tokens.
All inputs are finite; a program needn't handle non-finite values.
Results may differ from the reference program's by a relative error of at most 0.0054.
Values may be sent and summed in bfloat16 or wider, within the bound.
A program may use at most 64 MiB of HBM per device.

```python
import math
import jax
import jax.numpy as jnp
import numpy as np
from jax import lax

QUERY_HEAD_COUNT = 32
KEY_VALUE_HEADS = 4
HEAD_SIZE = 128
REACH = 1
CONTEXT_TOKENS = 256
PACKED_TOKENS = 4096
MOST = 257
NDOC = 32
N_CTX = 16


def draw_keys(key, part):
    drawn_result = jnp.clip(jax.random.normal(jax.random.fold_in(key, 3), (PACKED_TOKENS, KEY_VALUE_HEADS * HEAD_SIZE), jnp.float32), -6.0, 6.0)
    return drawn_result.astype(jnp.bfloat16)


def draw_queries(key, part):
    drawn_result = jnp.clip(jax.random.normal(jax.random.fold_in(key, 4), (PACKED_TOKENS, QUERY_HEAD_COUNT * HEAD_SIZE), jnp.float32), -6.0, 6.0)
    return drawn_result.astype(jnp.bfloat16)


def block_levels(own_key, dims, cuts, smallest, high):
    gain = 1.0
    for position, parts in cuts:
        draws = jax.random.uniform(jax.random.fold_in(jax.random.fold_in(own_key, 6), position), (parts,), jnp.float32, smallest / len(cuts), high / len(cuts))
        gain = gain * jnp.repeat(jnp.exp(draws), dims[position] // parts).reshape((-1,) + (1,) * (len(dims) - 1 - position))
    return gain


def length_profile(number_of, total, bound, skew):
    loads = [(1 << 20) // math.isqrt(rank ** skew) + 1 for rank in range(2, number_of + 1)]
    spare, counts = total - bound - (number_of - 1), [1] * (number_of - 1)
    while spare > 0:
        movable = [i for i in range(number_of - 1) if counts[i] < bound]
        pool, left = sum([loads[i] for i in movable]), spare
        for i in movable:
            extra = min(bound - counts[i], max(1, left * loads[i] // pool), spare)
            counts[i] = counts[i] + extra
            spare = spare - extra
    return np.array([bound] + counts)


def ragged_sizes(rng, amount, total, bound, slope):
    if amount == 2:
        one = jax.random.randint(rng, (), max(1, total - bound), min(bound, total - 1) + 1)
        return jnp.stack([one, total - one])
    lengths = jnp.asarray(length_profile(amount, total, bound, slope), jnp.int32)
    couples = (amount - 1) // 2
    giver, taker = lengths[1:1 + 2 * couples:2], lengths[2:2 + 2 * couples:2]
    margin = jnp.minimum(giver - 1, bound - taker)
    moved = jax.random.randint(jax.random.fold_in(rng, 1), (couples,), 0, 1 << 20) % (margin + 1)
    lengths = lengths.at[1:1 + 2 * couples:2].set(giver - moved).at[2:2 + 2 * couples:2].set(taker + moved)
    return lengths[jax.random.permutation(jax.random.fold_in(rng, 2), amount)]


def normal_values(rng, extent, deviation, bound, shards=(), kind=jnp.bfloat16):
    drawn = deviation * jax.random.normal(rng, extent, jnp.float32)
    if shards:
        drawn = drawn * block_levels(rng, extent, shards, -0.22, 0.18)
    return jnp.clip(drawn, -bound, bound).astype(kind)


def setup_inputs(seed: int = 0) -> dict:
    key_of = jax.random.split(jax.random.key(seed), 7)
    queries = draw_queries(jax.random.fold_in(key_of[6], 71), 0)
    keys = draw_keys(jax.random.fold_in(key_of[6], 71), 0)
    values = normal_values(key_of[2], (PACKED_TOKENS, KEY_VALUE_HEADS * HEAD_SIZE), 1.0, 6.0, ((0, 32),))
    attn_out = normal_values(key_of[3], (PACKED_TOKENS, QUERY_HEAD_COUNT * HEAD_SIZE), 1.0, 6.0, ((0, 32),))
    output_gradient = normal_values(key_of[4], (PACKED_TOKENS, QUERY_HEAD_COUNT * HEAD_SIZE), 1.0, 6.0, ((0, 32),))
    doc_lengths = ragged_sizes(key_of[5], NDOC, PACKED_TOKENS, MOST, 2).astype(jnp.int32)
    return dict(queries=queries, keys=keys, values=values, attn_out=attn_out, output_gradient=output_gradient, doc_lengths=doc_lengths)


fill_value = -1e30


def segment_ids(doc_lengths, positions):
    ends = jnp.cumsum(doc_lengths).astype(jnp.int32)
    return jnp.sum((ends[None, :] <= positions[:, None]).astype(jnp.int32), axis=1, dtype=jnp.int32)


def round_low(array):
    return lax.optimization_barrier(array.astype(jnp.bfloat16)).astype(jnp.float32)


def reference(queries, keys, values, attn_out, output_gradient, doc_lengths):
    group_width = QUERY_HEAD_COUNT // KEY_VALUE_HEADS
    score_scale = HEAD_SIZE ** -0.5
    width = (REACH + 1) * CONTEXT_TOKENS
    margin_amount = REACH * CONTEXT_TOKENS
    delta_value = jnp.sum((output_gradient.astype(jnp.float32) * attn_out.astype(jnp.float32)).reshape(PACKED_TOKENS, QUERY_HEAD_COUNT, HEAD_SIZE), axis=2).astype(jnp.bfloat16)
    seg_all = segment_ids(doc_lengths, jnp.arange(PACKED_TOKENS, dtype=jnp.int32))
    seg_pad = jnp.concatenate([jnp.full((margin_amount,), -1, jnp.int32), seg_all])
    pos_pad = jnp.arange(PACKED_TOKENS + margin_amount, dtype=jnp.int32) - margin_amount
    padded_keys = jnp.pad(keys.reshape(PACKED_TOKENS, KEY_VALUE_HEADS, HEAD_SIZE), ((margin_amount, 0), (0, 0), (0, 0)))
    padded_values = jnp.pad(values.reshape(PACKED_TOKENS, KEY_VALUE_HEADS, HEAD_SIZE), ((margin_amount, 0), (0, 0), (0, 0)))

    def block(carry, block_index):
        key_running_sum, value_running_sum = carry
        start_index = (block_index * CONTEXT_TOKENS).astype(jnp.int32)
        query_row_block = lax.dynamic_slice_in_dim(queries, start_index, CONTEXT_TOKENS, 0).reshape(CONTEXT_TOKENS, KEY_VALUE_HEADS, group_width, HEAD_SIZE).astype(jnp.float32)
        gradient_row_block = lax.dynamic_slice_in_dim(output_gradient, start_index, CONTEXT_TOKENS, 0).reshape(CONTEXT_TOKENS, KEY_VALUE_HEADS, group_width, HEAD_SIZE).astype(jnp.float32)
        row_delta_values = lax.dynamic_slice_in_dim(delta_value, start_index, CONTEXT_TOKENS, 0).reshape(CONTEXT_TOKENS, KEY_VALUE_HEADS, group_width).astype(jnp.float32)
        row_delta_values = jnp.transpose(row_delta_values, (1, 2, 0))
        key_rows = lax.dynamic_slice_in_dim(padded_keys, start_index, width, 0).astype(jnp.float32)
        value_rows = lax.dynamic_slice_in_dim(padded_values, start_index, width, 0).astype(jnp.float32)
        seg_query = lax.dynamic_slice_in_dim(seg_all, start_index, CONTEXT_TOKENS, 0)
        seg_key = lax.dynamic_slice_in_dim(seg_pad, start_index, width, 0)
        pos_query = start_index + jnp.arange(CONTEXT_TOKENS, dtype=jnp.int32)
        pos_key = lax.dynamic_slice_in_dim(pos_pad, start_index, width, 0)
        allowed = (seg_query[:, None] == seg_key[None, :]) & (pos_key[None, :] <= pos_query[:, None])
        scores = jnp.einsum('tkgd,ukd->kgtu', query_row_block, key_rows, precision=lax.Precision.HIGHEST) * score_scale
        masked = jnp.where(allowed, scores, fill_value)
        row_max = jnp.max(masked, axis=-1)
        row_sum = jnp.sum(jnp.where(allowed, jnp.exp(masked - row_max[..., None]), 0.0), axis=-1)
        lse = row_max + jnp.log(row_sum)
        probs = jnp.where(allowed, jnp.exp(jnp.where(allowed, scores - lse[..., None], fill_value)), 0.0)
        probs_low = round_low(probs)
        prob_grad = jnp.einsum('tkgd,ukd->kgtu', gradient_row_block, value_rows, precision=lax.Precision.HIGHEST)
        score_grad = round_low(probs * (prob_grad - row_delta_values[..., None]))
        query_part = jnp.einsum('kgtu,ukd->tkgd', score_grad, key_rows, precision=lax.Precision.HIGHEST) * score_scale
        key_part = jnp.einsum('kgtu,tkgd->ukd', score_grad, query_row_block, precision=lax.Precision.HIGHEST) * score_scale
        value_part = jnp.einsum('kgtu,tkgd->ukd', probs_low, gradient_row_block, precision=lax.Precision.HIGHEST)
        key_running_sum = lax.dynamic_update_slice_in_dim(key_running_sum, lax.dynamic_slice_in_dim(key_running_sum, start_index, width, 0) + key_part, start_index, 0)
        value_running_sum = lax.dynamic_update_slice_in_dim(value_running_sum, lax.dynamic_slice_in_dim(value_running_sum, start_index, width, 0) + value_part, start_index, 0)
        return (key_running_sum, value_running_sum), query_part.reshape(CONTEXT_TOKENS, QUERY_HEAD_COUNT * HEAD_SIZE).astype(jnp.bfloat16)

    zero_running_sum = jnp.zeros((PACKED_TOKENS + margin_amount, KEY_VALUE_HEADS, HEAD_SIZE), jnp.float32)
    (key_running_sum, value_running_sum), query_blocks = lax.scan(block, (zero_running_sum, zero_running_sum), jnp.arange(N_CTX, dtype=jnp.int32))
    query_grad = query_blocks.reshape(PACKED_TOKENS, QUERY_HEAD_COUNT * HEAD_SIZE)
    key_gradient = key_running_sum[margin_amount:].reshape(PACKED_TOKENS, KEY_VALUE_HEADS * HEAD_SIZE).astype(jnp.bfloat16)
    value_gradient = value_running_sum[margin_amount:].reshape(PACKED_TOKENS, KEY_VALUE_HEADS * HEAD_SIZE).astype(jnp.bfloat16)
    return (query_grad, key_gradient, value_gradient)
```

```python
import functools
import math

import jax
import jax.numpy as jnp
from jax import lax
from jax.experimental import pallas as pl
from jax.experimental.pallas import tpu as pltpu
from jax.sharding import PartitionSpec as P

HEAD_SIZE = 128
KEY_VALUE_HEADS = 4
WINDOW_SHARDS = 2
fill_value = -1e30
MESH = pl.DeviceIdType.MESH
NT = (((1,), (1,)), ((), ()))
TN = (((0,), (0,)), ((), ()))


def kernel(
    n_ctx, n_head, group, kv_heads,
    doc_ref, q_hbm, k_hbm, v_hbm, o_hbm, g_hbm,
    dq_hbm, dk_hbm, dv_hbm,
    qv, gv, ov, dqv, kw, vw, dlt, bias, p_buf, s_buf,
    own_dk, own_dv, send_dk, send_dv, got_dk, got_dv, out_dk, out_dv,
    in_sem, kv_sem, out_sem, fwd_send, fwd_recv, ret_send, ret_recv,
):
    d = HEAD_SIZE
    rows = q_hbm.shape[0]
    wide = group * d
    count = n_ctx * n_head
    back = WINDOW_SHARDS
    me = lax.axis_index("ctx") * n_head + lax.axis_index("head")
    scale = d ** -0.5

    def device(index):
        return {"ctx": index // n_head, "head": lax.rem(index, n_head)}

    def load(g):
        cols = pl.ds(g * wide, wide)
        return [
            pltpu.make_async_copy(g_hbm.at[:, cols], gv.at[g], in_sem.at[0, g]),
            pltpu.make_async_copy(o_hbm.at[:, cols], ov.at[g], in_sem.at[1, g]),
            pltpu.make_async_copy(q_hbm.at[:, cols], qv.at[g], in_sem.at[2, g]),
        ]

    def load_kv(g):
        cols = pl.ds(g * d, d)
        here = pl.ds(back * rows, rows)
        return [
            pltpu.make_async_copy(k_hbm.at[:, cols], kw.at[g, here], kv_sem.at[0, g]),
            pltpu.make_async_copy(v_hbm.at[:, cols], vw.at[g, here], kv_sem.at[1, g]),
        ]

    def forward(g, j):
        cols = pl.ds(pl.multiple_of(g * d, d), d)
        there = pl.ds((back - j) * rows, rows)
        target = device(lax.rem(me + j, count))
        return [
            pltpu.make_async_remote_copy(
                src_ref=src.at[:, cols], dst_ref=dst.at[g, there],
                send_sem=fwd_send.at[j - 1, i, g], recv_sem=fwd_recv.at[j - 1, i, g],
                device_id=target, device_id_type=MESH,
            )
            for i, (src, dst) in enumerate(((k_hbm, kw), (v_hbm, vw)))
        ]

    def give_back(g, j):
        there = pl.ds((back - j) * rows, rows)
        target = device(lax.rem(me - j + count, count))
        return [
            pltpu.make_async_remote_copy(
                src_ref=src.at[g, there], dst_ref=dst.at[j - 1, g],
                send_sem=ret_send.at[j - 1, i, g], recv_sem=ret_recv.at[j - 1, i, g],
                device_id=target, device_id_type=MESH,
            )
            for i, (src, dst) in enumerate(((send_dk, got_dk), (send_dv, got_dv)))
        ]

    for g in range(kv_heads):
        for copy in load(g) + load_kv(g):
            copy.start()

    barrier = pltpu.get_barrier_semaphore()
    peers = jnp.int32(0)
    for j in range(1, back + 1):
        @pl.when(me + j < count)
        def _():
            pl.semaphore_signal(
                barrier, inc=1, device_id=device(me + j), device_id_type=MESH
            )

        @pl.when(me - j >= 0)
        def _():
            pl.semaphore_signal(
                barrier, inc=1, device_id=device(me - j), device_id_type=MESH
            )

        peers = peers + (me + j < count).astype(jnp.int32) + (me - j >= 0).astype(jnp.int32)
    pl.semaphore_wait(barrier, peers)

    for g in range(kv_heads):
        for j in range(1, back + 1):
            @pl.when(me + j < count)
            def _():
                for copy in forward(g, j):
                    copy.start()

    for j in range(1, back + 1):
        @pl.when(me - j < 0)
        def _():
            there = pl.ds((back - j) * rows, rows)
            zero = jnp.zeros((kv_heads, rows, d), jnp.bfloat16)
            kw[:, there, :] = zero
            vw[:, there, :] = zero

        @pl.when(me + j >= count)
        def _():
            zero = jnp.zeros((kv_heads, rows, d), jnp.bfloat16)
            got_dk[j - 1] = zero
            got_dv[j - 1] = zero

    window = (back + 1) * rows
    first = me * rows
    here_t = first + lax.broadcasted_iota(jnp.int32, (8, rows), 1)

    def document(index, state):
        end, start = state
        end = end + doc_ref[index]
        return end, jnp.where(end <= here_t, end, start)

    start = lax.fori_loop(
        0, doc_ref.shape[0], document,
        (jnp.int32(0), jnp.zeros((8, rows), jnp.int32)), unroll=8,
    )[1][:1]
    pos_u = first - back * rows + lax.broadcasted_iota(jnp.int32, (window, rows), 0)
    pos_t = first + lax.broadcasted_iota(jnp.int32, (window, rows), 1)
    allowed = (pos_u <= pos_t) & (pos_u >= start)
    bias[...] = jnp.where(allowed, 0.0, fill_value).astype(jnp.float32)

    lane = lax.broadcasted_iota(jnp.int32, (rows, d), 1)

    def delta_of(g, carry):
        for copy in load(g)[:2]:
            copy.wait()
        for h in range(group):
            cols = slice(h * d, (h + 1) * d)
            product = gv[g, :, cols].astype(jnp.float32) * ov[g, :, cols].astype(jnp.float32)
            delta = jnp.sum(product, axis=1, keepdims=True)
            dlt[g, :, cols] = jnp.where(lane == 0, delta, 0.0).astype(jnp.bfloat16)
        return carry

    lax.fori_loop(0, kv_heads, delta_of, 0)

    minus = jnp.where(
        lax.broadcasted_iota(jnp.int32, (window, d), 1) == 0, -1.0, 0.0
    ).astype(jnp.bfloat16)
    factor = scale * math.log2(math.e)
    step = 2

    def one_group(g, carry):
        load(g)[2].wait()
        for copy in load_kv(g):
            copy.wait()
        for j in range(1, back + 1):
            @pl.when(me - j >= 0)
            def _():
                for copy in forward(g, j):
                    copy.wait_recv()

        k_all = kw[g]
        v_aug = jnp.concatenate([vw[g], minus], axis=1)

        def stack(ref, heads):
            return jnp.concatenate([ref[g, :, h * d : (h + 1) * d] for h in heads], axis=0)

        for pair in range(group // step):
            heads = range(pair * step, (pair + 1) * step)
            q_rows = stack(qv, heads)
            g_aug = jnp.concatenate([stack(gv, heads), stack(dlt, heads)], axis=1)
            scores = lax.dot_general(k_all, q_rows, NT, preferred_element_type=jnp.float32)
            scores = scores * factor + jnp.concatenate([bias[...]] * step, axis=1)
            top = jnp.max(scores, axis=0, keepdims=True)
            grown = jnp.exp2(scores - top)
            inverse = 1.0 / jnp.sum(grown, axis=0, keepdims=True)
            probs = grown * inverse
            cols = slice(pair * step * rows, (pair + 1) * step * rows)
            p_buf[:, cols] = probs.astype(jnp.bfloat16)
            diff = lax.dot_general(v_aug, g_aug, NT, preferred_element_type=jnp.float32)
            s_buf[:, cols] = (probs * diff).astype(jnp.bfloat16)

        dv = jnp.dot(
            p_buf[...], stack(gv, range(group)), preferred_element_type=jnp.float32
        )
        dk = (
            jnp.dot(s_buf[...], stack(qv, range(group)), preferred_element_type=jnp.float32)
            * scale
        )
        far = back * rows
        send_dk[g] = dk[:far].astype(jnp.bfloat16)
        send_dv[g] = dv[:far].astype(jnp.bfloat16)
        for j in range(1, back + 1):
            @pl.when(me - j >= 0)
            def _():
                for copy in give_back(g, j):
                    copy.start()
        own_dk[g] = dk[far:]
        own_dv[g] = dv[far:]
        dq = lax.dot_general(k_all, s_buf[...], TN, preferred_element_type=jnp.float32) * scale
        for h in range(group):
            piece = dq[:, h * rows : (h + 1) * rows]
            dqv[g, :, h * d : (h + 1) * d] = piece.T.astype(jnp.bfloat16)
        put_dq(g).start()
        return carry

    def put_dq(g):
        cols = pl.ds(pl.multiple_of(g * wide, wide), wide)
        return pltpu.make_async_copy(dqv.at[g], dq_hbm.at[:, cols], out_sem.at[g])

    lax.fori_loop(0, kv_heads, one_group, 0)

    for g in range(kv_heads):
        for j in range(1, back + 1):
            @pl.when(me + j < count)
            def _():
                for copy in give_back(g, j):
                    copy.wait_recv()
        cols = slice(g * d, (g + 1) * d)
        dk, dv = own_dk[g], own_dv[g]
        for j in range(back):
            dk = dk + got_dk[j, g].astype(jnp.float32)
            dv = dv + got_dv[j, g].astype(jnp.float32)
        out_dk[:, cols] = dk.astype(jnp.bfloat16)
        out_dv[:, cols] = dv.astype(jnp.bfloat16)
    put_k = pltpu.make_async_copy(out_dk, dk_hbm, out_sem.at[kv_heads])
    put_v = pltpu.make_async_copy(out_dv, dv_hbm, out_sem.at[kv_heads + 1])
    put_k.start()
    put_v.start()
    for g in range(kv_heads):
        put_dq(g).wait()
        for j in range(1, back + 1):
            @pl.when(me + j < count)
            def _():
                for copy in forward(g, j):
                    copy.wait_send()

            @pl.when(me - j >= 0)
            def _():
                for copy in give_back(g, j):
                    copy.wait_send()
    put_k.wait()
    put_v.wait()


def on_device(n_ctx, n_head, queries, keys, values, attn_out, output_gradient, doc_lengths):
    d = HEAD_SIZE
    rows = queries.shape[0]
    kv_heads = keys.shape[1] // d
    group = queries.shape[1] // keys.shape[1]
    wide = group * d
    back = WINDOW_SHARDS
    window = (back + 1) * rows
    low, full = jnp.bfloat16, jnp.float32
    dma = pltpu.SemaphoreType.DMA
    any_space = pl.BlockSpec(memory_space=pl.ANY)
    return pl.pallas_call(
        functools.partial(kernel, n_ctx, n_head, group, kv_heads),
        out_shape=(
            jax.ShapeDtypeStruct(queries.shape, low),
            jax.ShapeDtypeStruct(keys.shape, low),
            jax.ShapeDtypeStruct(values.shape, low),
        ),
        in_specs=[pl.BlockSpec(memory_space=pltpu.SMEM)] + [any_space] * 5,
        out_specs=(any_space,) * 3,
        scratch_shapes=[
            pltpu.VMEM((kv_heads, rows, wide), low),
            pltpu.VMEM((kv_heads, rows, wide), low),
            pltpu.VMEM((kv_heads, rows, wide), low),
            pltpu.VMEM((kv_heads, rows, wide), low),
            pltpu.VMEM((kv_heads, window, d), low),
            pltpu.VMEM((kv_heads, window, d), low),
            pltpu.VMEM((kv_heads, rows, wide), low),
            pltpu.VMEM((window, rows), full),
            pltpu.VMEM((window, group * rows), low),
            pltpu.VMEM((window, group * rows), low),
            pltpu.VMEM((kv_heads, rows, d), full),
            pltpu.VMEM((kv_heads, rows, d), full),
            pltpu.VMEM((kv_heads, back * rows, d), low),
            pltpu.VMEM((kv_heads, back * rows, d), low),
            pltpu.VMEM((back, kv_heads, rows, d), low),
            pltpu.VMEM((back, kv_heads, rows, d), low),
            pltpu.VMEM((rows, kv_heads * d), low),
            pltpu.VMEM((rows, kv_heads * d), low),
            dma((3, kv_heads)),
            dma((2, kv_heads)),
            dma((kv_heads + 2,)),
            dma((back, 2, kv_heads)),
            dma((back, 2, kv_heads)),
            dma((back, 2, kv_heads)),
            dma((back, 2, kv_heads)),
        ],
        compiler_params=pltpu.CompilerParams(collective_id=0, has_side_effects=True),
        name="packed_attention_backward",
    )(doc_lengths, queries, keys, values, attn_out, output_gradient)


def solution(mesh):
    n_ctx, n_head = mesh.shape["ctx"], mesh.shape["head"]
    rows = P(("ctx", "head"), None)
    return jax.shard_map(
        functools.partial(on_device, n_ctx, n_head),
        mesh=mesh,
        in_specs=(rows,) * 5 + (P(),),
        out_specs=(rows,) * 3,
        check_vma=False,
    )
```

```python
import functools
import math

import jax
import jax.numpy as jnp
from jax import lax
from jax.experimental import pallas as pl
from jax.experimental.pallas import tpu as pltpu
from jax.sharding import PartitionSpec as P

HEAD_SIZE = 128
fill_value = -1e30
MESH = pl.DeviceIdType.MESH
NT = (((1,), (1,)), ((), ()))
TN = (((0,), (0,)), ((), ()))


def kernel(
    n_ctx, group, mine_count,
    doc_ref, q_hbm, k_hbm, v_hbm, o_hbm, g_hbm,
    dq_out, dk_out, dv_out,
    q_buf, g_buf, g_all, o_all, d_buf, d_send,
    kw, vw, bias, p_buf, s_buf, acc_k, acc_v, own_k, own_v,
    send_k, send_v, part_k, part_v, next_k, next_v, dq_buf, dq_got,
    in_sem, fwd_send, fwd_recv, ret_send, ret_recv, chip_send, chip_recv,
):
    d = HEAD_SIZE
    rows = q_hbm.shape[0]
    wide = group * d
    window = 3 * rows
    ctx = lax.axis_index("ctx")
    me = lax.axis_index("head")
    other = 1 - me
    scale = d ** -0.5
    has_next = ctx + 1 < n_ctx
    has_back = ctx >= 1
    following = lax.rem(ctx + 1, n_ctx)
    previous = lax.rem(ctx + n_ctx - 1, n_ctx)

    def block(index, width):
        return pl.ds(pl.multiple_of(index * width, width), width)

    def remote(src, dst, send, recv, where, head):
        return pltpu.make_async_remote_copy(
            src_ref=src, dst_ref=dst, send_sem=send, recv_sem=recv,
            device_id={"ctx": where, "head": head}, device_id_type=MESH,
        )

    def load_mine(i):
        cols = block(me * mine_count + i, d)
        here = block(2 + me, rows)
        return [
            pltpu.make_async_copy(
                q_hbm.at[:, block(me * mine_count + i, wide)], q_buf.at[i, me], in_sem.at[0, i]
            ),
            pltpu.make_async_copy(
                g_hbm.at[:, block(me * mine_count + i, wide)], g_buf.at[i, me], in_sem.at[5, i]
            ),
            pltpu.make_async_copy(k_hbm.at[:, cols], kw.at[i, here], in_sem.at[1, i]),
            pltpu.make_async_copy(v_hbm.at[:, cols], vw.at[i, here], in_sem.at[2, i]),
        ]

    def load_all(g):
        cols = block(g, wide)
        return [
            pltpu.make_async_copy(g_hbm.at[:, cols], g_all.at[g], in_sem.at[3, g]),
            pltpu.make_async_copy(o_hbm.at[:, cols], o_all.at[g], in_sem.at[4, g]),
        ]

    def forward(i, source, head):
        cols = block(head * mine_count + i, d)
        return [
            remote(
                src.at[:, cols], dst.at[i, block(source, rows)],
                fwd_send.at[head, x, i], fwd_recv.at[source, x, i], following, head,
            )
            for x, (src, dst) in enumerate(((k_hbm, kw), (v_hbm, vw)))
        ]

    def give_back(i, source, head):
        return [
            remote(
                src.at[i, head], dst.at[source * mine_count + i],
                ret_send.at[head, x, i], ret_recv.at[source, x, i], previous, head,
            )
            for x, (src, dst) in enumerate(((send_k, next_k), (send_v, next_v)))
        ]

    def across(i, source):
        theirs = (1 - source) * mine_count + i
        cols = block(theirs, d)
        return [
            remote(
                src, dst, chip_send.at[x, i], chip_recv.at[x, i], ctx, 1 - source
            )
            for x, (src, dst) in enumerate((
                (k_hbm.at[:, cols], kw.at[i, block(2 + source, rows)]),
                (v_hbm.at[:, cols], vw.at[i, block(2 + source, rows)]),
                (q_hbm.at[:, block(theirs, wide)], q_buf.at[i, source]),
                (g_hbm.at[:, block(theirs, wide)], g_buf.at[i, source]),
                (d_send.at[i], d_buf.at[i, source]),
                (dq_buf.at[i, 1 - source], dq_got.at[i]),
                (send_k.at[i, 2], part_k.at[i]),
                (send_v.at[i, 2], part_v.at[i]),
            ))
        ]

    barrier = pltpu.get_barrier_semaphore()

    def greet(where, head):
        pl.semaphore_signal(
            barrier, inc=1, device_id={"ctx": where, "head": head}, device_id_type=MESH
        )

    greet(ctx, other)
    for head in range(2):
        @pl.when(has_next)
        def _():
            greet(following, head)

        @pl.when(has_back)
        def _():
            greet(previous, head)

    for i in range(mine_count):
        for copy in load_mine(i):
            copy.start()
    for g in range(2 * mine_count):
        for copy in load_all(g):
            copy.start()

    pl.semaphore_wait(
        barrier, 1 + 2 * has_next.astype(jnp.int32) + 2 * has_back.astype(jnp.int32)
    )

    for i in range(mine_count):
        @pl.when(has_next)
        def _():
            for head in range(2):
                for copy in forward(i, me, head):
                    copy.start()

        for copy in across(i, me)[:4]:
            copy.start()

    @pl.when(jnp.logical_not(has_back))
    def _():
        zero = jnp.zeros((mine_count, 2 * rows, d), jnp.bfloat16)
        kw[:, : 2 * rows, :] = zero
        vw[:, : 2 * rows, :] = zero

    @pl.when(jnp.logical_not(has_next))
    def _():
        next_k[...] = jnp.zeros(next_k.shape, jnp.bfloat16)
        next_v[...] = jnp.zeros(next_v.shape, jnp.bfloat16)

    lane = lax.broadcasted_iota(jnp.int32, (rows, d), 1)

    def delta_of(g):
        for copy in load_all(g):
            copy.wait()
        total = jnp.zeros((rows, d), jnp.float32)
        for h in range(group):
            cols = slice(h * d, (h + 1) * d)
            product = g_all[g, :, cols].astype(jnp.float32) * o_all[g, :, cols].astype(jnp.float32)
            total = jnp.where(lane == h, jnp.sum(product, axis=1, keepdims=True), total)
        return total.astype(jnp.bfloat16)

    for i in range(mine_count):
        d_send[i] = delta_of(other * mine_count + i)
        across(i, me)[4].start()

    for token_block in range(2):
        first = (2 * ctx + token_block) * rows
        here_t = first + lax.broadcasted_iota(jnp.int32, (8, rows), 1)

        def document(index, state):
            end, start = state
            end = end + doc_ref[index]
            return end, jnp.where(end <= here_t, end, start)

        start = lax.fori_loop(
            0, doc_ref.shape[0], document,
            (jnp.int32(0), jnp.zeros((8, rows), jnp.int32)), unroll=8,
        )[1][:1]
        pos_u = first - 2 * rows + lax.broadcasted_iota(jnp.int32, (window, rows), 0)
        pos_t = first + lax.broadcasted_iota(jnp.int32, (window, rows), 1)
        allowed = (pos_u <= pos_t) & (pos_u >= start)
        bias[token_block] = jnp.where(allowed, 0.0, fill_value).astype(jnp.float32)

    for i in range(mine_count):
        d_buf[i, me] = delta_of(me * mine_count + i)

    minus = jnp.full((window, d), -1.0, jnp.bfloat16)
    factor = scale * math.log2(math.e)
    step = 2

    def unit(i, token_block):
        span = slice(token_block * rows, token_block * rows + window)
        k_all = kw[i, span]
        v_aug = jnp.concatenate([vw[i, span], minus], axis=1)

        def stack(ref, heads):
            return jnp.concatenate(
                [ref[i, token_block, :, h * d : (h + 1) * d] for h in heads], axis=0
            )

        for pair in range(group // step):
            heads = range(pair * step, (pair + 1) * step)
            q_rows = stack(q_buf, heads)
            deltas = d_buf[i, token_block]
            zero = jnp.zeros_like(deltas)
            d_rows = jnp.concatenate([jnp.where(lane == h, deltas, zero) for h in heads], axis=0)
            g_aug = jnp.concatenate([stack(g_buf, heads), d_rows], axis=1)
            scores = lax.dot_general(k_all, q_rows, NT, preferred_element_type=jnp.float32)
            scores = scores * factor + jnp.concatenate([bias[token_block]] * step, axis=1)
            top = jnp.max(scores, axis=0, keepdims=True)
            grown = jnp.exp2(scores - top)
            inverse = 1.0 / jnp.sum(grown, axis=0, keepdims=True)
            probs = grown * inverse
            cols = slice(pair * step * rows, (pair + 1) * step * rows)
            p_buf[:, cols] = probs.astype(jnp.bfloat16)
            diff = lax.dot_general(v_aug, g_aug, NT, preferred_element_type=jnp.float32)
            s_buf[:, cols] = (probs * diff).astype(jnp.bfloat16)

        acc_v[span, :] += jnp.dot(
            p_buf[...], stack(g_buf, range(group)), preferred_element_type=jnp.float32
        )
        acc_k[span, :] += (
            jnp.dot(s_buf[...], stack(q_buf, range(group)), preferred_element_type=jnp.float32)
            * scale
        )

    def query_part(i, token_block):
        span = slice(token_block * rows, token_block * rows + window)
        dq = lax.dot_general(
            kw[i, span], s_buf[...], TN, preferred_element_type=jnp.float32
        ) * scale
        for h in range(group):
            piece = dq[:, h * rows : (h + 1) * rows].T.astype(jnp.bfloat16)
            dq_buf[i, token_block, :, h * d : (h + 1) * d] = piece

        @pl.when(me != token_block)
        def _():
            across(i, me)[5].start()

    def finish(i, head):
        for acc, send in ((acc_k, send_k), (acc_v, send_v)):
            send[i, head] = acc[head * rows : (head + 1) * rows].astype(jnp.bfloat16)

        @pl.when(has_back)
        def _():
            for copy in give_back(i, me, head):
                copy.start()

    def one_group(i):
        for copy in load_mine(i):
            copy.wait()
        for copy in across(i, other)[:5]:
            copy.wait_recv()

        @pl.when(has_back)
        def _():
            for source in range(2):
                for copy in forward(i, source, me):
                    copy.wait_recv()

        acc_k[...] = jnp.zeros(acc_k.shape, jnp.float32)
        acc_v[...] = jnp.zeros(acc_v.shape, jnp.float32)
        unit(i, 0)
        finish(i, 0)
        query_part(i, 0)
        unit(i, 1)
        finish(i, 1)
        for acc, send, own in ((acc_k, send_k, own_k), (acc_v, send_v, own_v)):
            send[i, 2] = acc[block(2 + other, rows), :].astype(jnp.bfloat16)
            own[i] = acc[block(2 + me, rows), :]
        for copy in across(i, me)[6:]:
            copy.start()
        query_part(i, 1)

    for i in range(mine_count):
        one_group(i)

    for i in range(mine_count):
        for copy in across(i, other)[5:]:
            copy.wait_recv()

        @pl.when(has_next)
        def _():
            for source in range(2):
                for copy in give_back(i, source, me):
                    copy.wait_recv()

        dq_out[:, block(other * mine_count + i, wide)] = dq_got[i]
        dq_out[:, block(me * mine_count + i, wide)] = dq_buf[i, me]
        for own, part, late, out in (
            (own_k, part_k, next_k, dk_out), (own_v, part_v, next_v, dv_out)
        ):
            g = me * mine_count + i
            total = own[i] + late[g].astype(jnp.float32)
            out[:, block(g, d)] = total.astype(jnp.bfloat16)
            g = other * mine_count + i
            total = part[i].astype(jnp.float32) + late[g].astype(jnp.float32)
            out[:, block(g, d)] = total.astype(jnp.bfloat16)

    for i in range(mine_count):
        for copy in across(i, me):
            copy.wait_send()

        @pl.when(has_next)
        def _():
            for head in range(2):
                for copy in forward(i, me, head):
                    copy.wait_send()

        @pl.when(has_back)
        def _():
            for head in range(2):
                for copy in give_back(i, me, head):
                    copy.wait_send()


def on_device(n_ctx, n_head, queries, keys, values, attn_out, output_gradient, doc_lengths):
    d = HEAD_SIZE
    rows = queries.shape[0]
    kv_heads = keys.shape[1] // d
    group = queries.shape[1] // keys.shape[1]
    wide = group * d
    mine = kv_heads // n_head
    low, full = jnp.bfloat16, jnp.float32
    dma = pltpu.SemaphoreType.DMA
    any_space = pl.BlockSpec(memory_space=pl.ANY)
    return pl.pallas_call(
        functools.partial(kernel, n_ctx, group, mine),
        out_shape=(
            pltpu.VMEM(queries.shape, low),
            pltpu.VMEM(keys.shape, low),
            pltpu.VMEM(values.shape, low),
        ),
        in_specs=[pl.BlockSpec(memory_space=pltpu.SMEM)] + [any_space] * 5,
        out_specs=(pl.BlockSpec(memory_space=pltpu.VMEM),) * 3,
        scratch_shapes=[
            pltpu.VMEM((mine, 2, rows, wide), low),
            pltpu.VMEM((mine, 2, rows, wide), low),
            pltpu.VMEM((kv_heads, rows, wide), low),
            pltpu.VMEM((kv_heads, rows, wide), low),
            pltpu.VMEM((mine, 2, rows, d), low),
            pltpu.VMEM((mine, rows, d), low),
            pltpu.VMEM((mine, 4 * rows, d), low),
            pltpu.VMEM((mine, 4 * rows, d), low),
            pltpu.VMEM((2, 3 * rows, rows), full),
            pltpu.VMEM((3 * rows, group * rows), low),
            pltpu.VMEM((3 * rows, group * rows), low),
            pltpu.VMEM((4 * rows, d), full),
            pltpu.VMEM((4 * rows, d), full),
            pltpu.VMEM((mine, rows, d), full),
            pltpu.VMEM((mine, rows, d), full),
            pltpu.VMEM((mine, 3, rows, d), low),
            pltpu.VMEM((mine, 3, rows, d), low),
            pltpu.VMEM((mine, rows, d), low),
            pltpu.VMEM((mine, rows, d), low),
            pltpu.VMEM((kv_heads, rows, d), low),
            pltpu.VMEM((kv_heads, rows, d), low),
            pltpu.VMEM((mine, 2, rows, wide), low),
            pltpu.VMEM((mine, rows, wide), low),
            dma((6, kv_heads)),
            dma((2, 2, mine)),
            dma((2, 2, mine)),
            dma((2, 2, mine)),
            dma((2, 2, mine)),
            dma((8, mine)),
            dma((8, mine)),
        ],
        compiler_params=pltpu.CompilerParams(collective_id=0, has_side_effects=True),
        name="packed_attention_backward",
    )(doc_lengths, queries, keys, values, attn_out, output_gradient)


def solution(mesh):
    n_ctx, n_head = mesh.shape["ctx"], mesh.shape["head"]
    rows = P(("ctx", "head"), None)
    return jax.shard_map(
        functools.partial(on_device, n_ctx, n_head),
        mesh=mesh,
        in_specs=(rows,) * 5 + (P(),),
        out_specs=(rows,) * 3,
        check_vma=False,
    )
```

```python
import functools
import math

import jax
import jax.numpy as jnp
from jax import lax
from jax.experimental import pallas as pl
from jax.experimental.pallas import tpu as pltpu
from jax.sharding import PartitionSpec as P

HEAD_SIZE = 128
fill_value = -1e30
MESH = pl.DeviceIdType.MESH
NT = (((1,), (1,)), ((), ()))
TN = (((0,), (0,)), ((), ()))


def kernel(
    n_ctx, group, mine_count,
    doc_ref, q_hbm, k_hbm, v_hbm, o_hbm, g_hbm,
    dq_out, dk_out, dv_out,
    q_buf, g_buf, g_all, o_all, d_buf, d_send,
    kw, vw, bias, p_buf, s_buf, acc_k, acc_v, near_k, near_v, own_k, own_v,
    send_k, send_v, part_k, part_v, next_k, next_v, dq_buf, dq_got,
    in_sem, fwd_send, fwd_recv, ret_send, ret_recv, chip_send, chip_recv,
):
    d = HEAD_SIZE
    rows = q_hbm.shape[0]
    wide = group * d
    window = 3 * rows
    ctx = lax.axis_index("ctx")
    me = lax.axis_index("head")
    other = 1 - me
    scale = d ** -0.5
    has_next = ctx + 1 < n_ctx
    has_back = ctx >= 1
    following = lax.rem(ctx + 1, n_ctx)
    previous = lax.rem(ctx + n_ctx - 1, n_ctx)

    def block(index, width):
        return pl.ds(pl.multiple_of(index * width, width), width)

    def remote(src, dst, send, recv, where, head):
        return pltpu.make_async_remote_copy(
            src_ref=src, dst_ref=dst, send_sem=send, recv_sem=recv,
            device_id={"ctx": where, "head": head}, device_id_type=MESH,
        )

    def load_mine(i):
        cols = block(me * mine_count + i, d)
        here = block(2 + me, rows)
        return [
            pltpu.make_async_copy(
                q_hbm.at[:, block(me * mine_count + i, wide)], q_buf.at[i, me], in_sem.at[0, i]
            ),
            pltpu.make_async_copy(
                g_hbm.at[:, block(me * mine_count + i, wide)], g_buf.at[i, me], in_sem.at[5, i]
            ),
            pltpu.make_async_copy(k_hbm.at[:, cols], kw.at[i, here], in_sem.at[1, i]),
            pltpu.make_async_copy(v_hbm.at[:, cols], vw.at[i, here], in_sem.at[2, i]),
        ]

    def load_all(g):
        cols = block(g, wide)
        return [
            pltpu.make_async_copy(g_hbm.at[:, cols], g_all.at[g], in_sem.at[3, g]),
            pltpu.make_async_copy(o_hbm.at[:, cols], o_all.at[g], in_sem.at[4, g]),
        ]

    def forward(i, source, head):
        cols = block(head * mine_count + i, d)
        return [
            remote(
                src.at[:, cols], dst.at[i, block(source, rows)],
                fwd_send.at[head, x, i], fwd_recv.at[source, x, i], following, head,
            )
            for x, (src, dst) in enumerate(((k_hbm, kw), (v_hbm, vw)))
        ]

    def give_back(i, source, head):
        return [
            remote(
                src.at[i, head], dst.at[source * mine_count + i],
                ret_send.at[head, x, i], ret_recv.at[source, x, i], previous, head,
            )
            for x, (src, dst) in enumerate(((send_k, next_k), (send_v, next_v)))
        ]

    def across(i, source):
        theirs = (1 - source) * mine_count + i
        cols = block(theirs, d)
        return [
            remote(
                src, dst, chip_send.at[x, i], chip_recv.at[x, i], ctx, 1 - source
            )
            for x, (src, dst) in enumerate((
                (k_hbm.at[:, cols], kw.at[i, block(2 + source, rows)]),
                (v_hbm.at[:, cols], vw.at[i, block(2 + source, rows)]),
                (q_hbm.at[:, block(theirs, wide)], q_buf.at[i, source]),
                (g_hbm.at[:, block(theirs, wide)], g_buf.at[i, source]),
                (d_send.at[i], d_buf.at[i, source]),
                (dq_buf.at[i, 1 - source], dq_got.at[i]),
                (send_k.at[i, 2], part_k.at[i]),
                (send_v.at[i, 2], part_v.at[i]),
            ))
        ]

    barrier = pltpu.get_barrier_semaphore()

    def greet(where, head):
        pl.semaphore_signal(
            barrier, inc=1, device_id={"ctx": where, "head": head}, device_id_type=MESH
        )

    greet(ctx, other)
    for head in range(2):
        @pl.when(has_next)
        def _():
            greet(following, head)

        @pl.when(has_back)
        def _():
            greet(previous, head)

    for i in range(mine_count):
        for copy in load_mine(i):
            copy.start()
    for g in range(2 * mine_count):
        for copy in load_all(g):
            copy.start()

    pl.semaphore_wait(
        barrier, 1 + 2 * has_next.astype(jnp.int32) + 2 * has_back.astype(jnp.int32)
    )

    for i in range(mine_count):
        @pl.when(has_next)
        def _():
            for head in range(2):
                for copy in forward(i, me, head):
                    copy.start()

        for copy in across(i, me)[:4]:
            copy.start()

    @pl.when(jnp.logical_not(has_back))
    def _():
        zero = jnp.zeros((mine_count, 2 * rows, d), jnp.bfloat16)
        kw[:, : 2 * rows, :] = zero
        vw[:, : 2 * rows, :] = zero

    @pl.when(jnp.logical_not(has_next))
    def _():
        next_k[...] = jnp.zeros(next_k.shape, jnp.bfloat16)
        next_v[...] = jnp.zeros(next_v.shape, jnp.bfloat16)

    lane = lax.broadcasted_iota(jnp.int32, (rows, d), 1)

    def delta_of(g):
        for copy in load_all(g):
            copy.wait()
        total = jnp.zeros((rows, d), jnp.float32)
        for h in range(group):
            cols = slice(h * d, (h + 1) * d)
            product = g_all[g, :, cols].astype(jnp.float32) * o_all[g, :, cols].astype(jnp.float32)
            total = jnp.where(lane == h, jnp.sum(product, axis=1, keepdims=True), total)
        return total.astype(jnp.bfloat16)

    for i in range(mine_count):
        d_send[i] = delta_of(other * mine_count + i)
        across(i, me)[4].start()

    for token_block in range(2):
        first = (2 * ctx + token_block) * rows
        here_t = first + lax.broadcasted_iota(jnp.int32, (8, rows), 1)

        def document(index, state):
            end, start = state
            end = end + doc_ref[index]
            return end, jnp.where(end <= here_t, end, start)

        start = lax.fori_loop(
            0, doc_ref.shape[0], document,
            (jnp.int32(0), jnp.zeros((8, rows), jnp.int32)), unroll=8,
        )[1][:1]
        pos_u = first - 2 * rows + lax.broadcasted_iota(jnp.int32, (window, rows), 0)
        pos_t = first + lax.broadcasted_iota(jnp.int32, (window, rows), 1)
        allowed = (pos_u <= pos_t) & (pos_u >= start)
        bias[token_block] = jnp.where(allowed, 0.0, fill_value).astype(jnp.float32)

    for i in range(mine_count):
        d_buf[i, me] = delta_of(me * mine_count + i)

    minus = jnp.full((window, d), -1.0, jnp.bfloat16)
    factor = scale * math.log2(math.e)
    step = 2

    def unit(i, token_block):
        span = slice(token_block * rows, token_block * rows + window)
        k_all = kw[i, span]
        v_aug = jnp.concatenate([vw[i, span], minus], axis=1)

        for pair in range(group // step):
            heads = range(pair * step, (pair + 1) * step)
            q_rows = stack(q_buf, i, token_block, heads)
            deltas = d_buf[i, token_block]
            zero = jnp.zeros_like(deltas)
            d_rows = jnp.concatenate([jnp.where(lane == h, deltas, zero) for h in heads], axis=0)
            g_aug = jnp.concatenate([stack(g_buf, i, token_block, heads), d_rows], axis=1)
            scores = lax.dot_general(k_all, q_rows, NT, preferred_element_type=jnp.float32)
            scores = scores * factor + jnp.concatenate([bias[token_block]] * step, axis=1)
            top = jnp.max(scores, axis=0, keepdims=True)
            grown = jnp.exp2(scores - top)
            inverse = 1.0 / jnp.sum(grown, axis=0, keepdims=True)
            probs = grown * inverse
            cols = slice(pair * step * rows, (pair + 1) * step * rows)
            p_buf[i, token_block, :, cols] = probs.astype(jnp.bfloat16)
            diff = lax.dot_general(v_aug, g_aug, NT, preferred_element_type=jnp.float32)
            s_buf[i, token_block, :, cols] = (probs * diff).astype(jnp.bfloat16)

    def stack(ref, i, token_block, heads):
        return jnp.concatenate(
            [ref[i, token_block, :, h * d : (h + 1) * d] for h in heads], axis=0
        )

    def key_sum(buf, ref, i, token_block, low, high):
        return jnp.dot(
            buf[i, token_block, low:high], stack(ref, i, token_block, range(group)),
            preferred_element_type=jnp.float32,
        )

    def far_part(i, token_block):
        for buf, ref, send, carry, factor_out in (
            (s_buf, q_buf, send_k, acc_k, scale), (p_buf, g_buf, send_v, acc_v, None)
        ):
            total = key_sum(buf, ref, i, token_block, 0, (2 - token_block) * rows)
            if token_block == 0:
                carry[...] = total[rows:]
                total = total[:rows]
            else:
                total = total + carry[...]
            if factor_out is not None:
                total = total * factor_out
            send[i, token_block] = total.astype(jnp.bfloat16)

        @pl.when(has_back)
        def _():
            for copy in give_back(i, me, token_block):
                copy.start()

    def near_part(i):
        for buf, ref, send, own, near, factor_out in (
            (s_buf, q_buf, send_k, own_k, near_k, scale),
            (p_buf, g_buf, send_v, own_v, near_v, None),
        ):
            early = key_sum(buf, ref, i, 0, 2 * rows, 3 * rows)
            late = key_sum(buf, ref, i, 1, rows, 3 * rows)
            if factor_out is not None:
                early, late = early * factor_out, late * factor_out
            near[0] = early + late[:rows]
            near[1] = late[rows:]
            send[i, 2] = near[other].astype(jnp.bfloat16)
            own[i] = near[me]
        for copy in across(i, me)[6:]:
            copy.start()

    def query_part(i, token_block):
        span = slice(token_block * rows, token_block * rows + window)
        dq = lax.dot_general(
            kw[i, span], s_buf[i, token_block], TN, preferred_element_type=jnp.float32
        ) * scale
        for h in range(group):
            piece = dq[:, h * rows : (h + 1) * rows].T.astype(jnp.bfloat16)
            dq_buf[i, token_block, :, h * d : (h + 1) * d] = piece

        @pl.when(me != token_block)
        def _():
            across(i, me)[5].start()

    def one_group(i):
        for copy in load_mine(i):
            copy.wait()
        for copy in across(i, other)[:5]:
            copy.wait_recv()

        @pl.when(has_back)
        def _():
            for source in range(2):
                for copy in forward(i, source, me):
                    copy.wait_recv()

        for token_block in range(2):
            unit(i, token_block)
            far_part(i, token_block)

    for i in range(mine_count):
        one_group(i)
    for i in range(mine_count):
        near_part(i)
        for token_block in range(2):
            query_part(i, token_block)

    for i in range(mine_count):
        for copy in across(i, other)[5:]:
            copy.wait_recv()

        @pl.when(has_next)
        def _():
            for source in range(2):
                for copy in give_back(i, source, me):
                    copy.wait_recv()

        dq_out[:, block(other * mine_count + i, wide)] = dq_got[i]
        dq_out[:, block(me * mine_count + i, wide)] = dq_buf[i, me]
        for own, part, late, out in (
            (own_k, part_k, next_k, dk_out), (own_v, part_v, next_v, dv_out)
        ):
            g = me * mine_count + i
            total = own[i] + late[g].astype(jnp.float32)
            out[:, block(g, d)] = total.astype(jnp.bfloat16)
            g = other * mine_count + i
            total = part[i].astype(jnp.float32) + late[g].astype(jnp.float32)
            out[:, block(g, d)] = total.astype(jnp.bfloat16)

    for i in range(mine_count):
        for copy in across(i, me):
            copy.wait_send()

        @pl.when(has_next)
        def _():
            for head in range(2):
                for copy in forward(i, me, head):
                    copy.wait_send()

        @pl.when(has_back)
        def _():
            for head in range(2):
                for copy in give_back(i, me, head):
                    copy.wait_send()


def store_kernel(dq, dk, dv, dq_hbm, dk_hbm, dv_hbm, sem):
    copies = [
        pltpu.make_async_copy(src, dst, sem.at[x])
        for x, (src, dst) in enumerate(((dq, dq_hbm), (dk, dk_hbm), (dv, dv_hbm)))
    ]
    for copy in copies:
        copy.start()
    for copy in copies:
        copy.wait()


def on_device(n_ctx, n_head, queries, keys, values, attn_out, output_gradient, doc_lengths):
    d = HEAD_SIZE
    rows = queries.shape[0]
    kv_heads = keys.shape[1] // d
    group = queries.shape[1] // keys.shape[1]
    wide = group * d
    mine = kv_heads // n_head
    low, full = jnp.bfloat16, jnp.float32
    dma = pltpu.SemaphoreType.DMA
    any_space = pl.BlockSpec(memory_space=pl.ANY)
    results = pl.pallas_call(
        functools.partial(kernel, n_ctx, group, mine),
        out_shape=(
            pltpu.VMEM(queries.shape, low),
            pltpu.VMEM(keys.shape, low),
            pltpu.VMEM(values.shape, low),
        ),
        in_specs=[pl.BlockSpec(memory_space=pltpu.SMEM)] + [any_space] * 5,
        out_specs=(pl.BlockSpec(memory_space=pltpu.VMEM),) * 3,
        scratch_shapes=[
            pltpu.VMEM((mine, 2, rows, wide), low),
            pltpu.VMEM((mine, 2, rows, wide), low),
            pltpu.VMEM((kv_heads, rows, wide), low),
            pltpu.VMEM((kv_heads, rows, wide), low),
            pltpu.VMEM((mine, 2, rows, d), low),
            pltpu.VMEM((mine, rows, d), low),
            pltpu.VMEM((mine, 4 * rows, d), low),
            pltpu.VMEM((mine, 4 * rows, d), low),
            pltpu.VMEM((2, 3 * rows, rows), full),
            pltpu.VMEM((mine, 2, 3 * rows, group * rows), low),
            pltpu.VMEM((mine, 2, 3 * rows, group * rows), low),
            pltpu.VMEM((rows, d), full),
            pltpu.VMEM((rows, d), full),
            pltpu.VMEM((2, rows, d), full),
            pltpu.VMEM((2, rows, d), full),
            pltpu.VMEM((mine, rows, d), full),
            pltpu.VMEM((mine, rows, d), full),
            pltpu.VMEM((mine, 3, rows, d), low),
            pltpu.VMEM((mine, 3, rows, d), low),
            pltpu.VMEM((mine, rows, d), low),
            pltpu.VMEM((mine, rows, d), low),
            pltpu.VMEM((kv_heads, rows, d), low),
            pltpu.VMEM((kv_heads, rows, d), low),
            pltpu.VMEM((mine, 2, rows, wide), low),
            pltpu.VMEM((mine, rows, wide), low),
            dma((6, kv_heads)),
            dma((2, 2, mine)),
            dma((2, 2, mine)),
            dma((2, 2, mine)),
            dma((2, 2, mine)),
            dma((8, mine)),
            dma((8, mine)),
        ],
        compiler_params=pltpu.CompilerParams(collective_id=0, has_side_effects=True),
        name="packed_attention_backward",
    )(doc_lengths, queries, keys, values, attn_out, output_gradient)
    return pl.pallas_call(
        store_kernel,
        out_shape=tuple(jax.ShapeDtypeStruct(r.shape, low) for r in results),
        in_specs=[pl.BlockSpec(memory_space=pltpu.VMEM)] * 3,
        out_specs=(any_space,) * 3,
        scratch_shapes=[dma((3,))],
        name="store_gradients",
    )(*[pltpu.with_memory_space_constraint(r, pltpu.VMEM) for r in results])


def solution(mesh):
    n_ctx, n_head = mesh.shape["ctx"], mesh.shape["head"]
    rows = P(("ctx", "head"), None)
    return jax.shard_map(
        functools.partial(on_device, n_ctx, n_head),
        mesh=mesh,
        in_specs=(rows,) * 5 + (P(),),
        out_specs=(rows,) * 3,
        check_vma=False,
    )
```

```python
import functools
import math

import jax
import jax.numpy as jnp
from jax import lax
from jax.experimental import pallas as pl
from jax.experimental.pallas import tpu as pltpu
from jax.sharding import PartitionSpec as P

HEAD_SIZE = 128
fill_value = -1e30
MESH = pl.DeviceIdType.MESH
NT = (((1,), (1,)), ((), ()))
TN = (((0,), (0,)), ((), ()))


def kernel(
    n_ctx, group, mine_count,
    doc_ref, q_hbm, k_hbm, v_hbm, o_hbm, g_hbm,
    dq_out, dk_out, dv_out,
    q_buf, g_buf, g_all, o_all, d_buf, d_send,
    kw, vw, bias, p_buf, s_buf, acc_k, acc_v, near_k, near_v, own_k, own_v,
    send_k, send_v, part_k, part_v, next_k, next_v, dq_buf, dq_got,
    in_sem, fwd_send, fwd_recv, ret_send, ret_recv, chip_send, chip_recv,
):
    d = HEAD_SIZE
    rows = q_hbm.shape[0]
    wide = group * d
    window = 3 * rows
    ctx = lax.axis_index("ctx")
    me = lax.axis_index("head")
    other = 1 - me
    scale = d ** -0.5
    has_next = ctx + 1 < n_ctx
    has_back = ctx >= 1
    following = lax.rem(ctx + 1, n_ctx)
    previous = lax.rem(ctx + n_ctx - 1, n_ctx)

    def block(index, width):
        return pl.ds(pl.multiple_of(index * width, width), width)

    def remote(src, dst, send, recv, where, head):
        return pltpu.make_async_remote_copy(
            src_ref=src, dst_ref=dst, send_sem=send, recv_sem=recv,
            device_id={"ctx": where, "head": head}, device_id_type=MESH,
        )

    def load_mine(i):
        cols = block(me * mine_count + i, d)
        here = block(2 + me, rows)
        return [
            pltpu.make_async_copy(
                q_hbm.at[:, block(me * mine_count + i, wide)], q_buf.at[i, me], in_sem.at[0, i]
            ),
            pltpu.make_async_copy(
                g_hbm.at[:, block(me * mine_count + i, wide)], g_buf.at[i, me], in_sem.at[5, i]
            ),
            pltpu.make_async_copy(k_hbm.at[:, cols], kw.at[i, here], in_sem.at[1, i]),
            pltpu.make_async_copy(v_hbm.at[:, cols], vw.at[i, here], in_sem.at[2, i]),
        ]

    def load_all(g):
        cols = block(g, wide)
        return [
            pltpu.make_async_copy(g_hbm.at[:, cols], g_all.at[g], in_sem.at[3, g]),
            pltpu.make_async_copy(o_hbm.at[:, cols], o_all.at[g], in_sem.at[4, g]),
        ]

    def forward(i, source, head):
        cols = block(head * mine_count + i, d)
        return [
            remote(
                src.at[:, cols], dst.at[i, block(source, rows)],
                fwd_send.at[head, x, i], fwd_recv.at[source, x, i], following, head,
            )
            for x, (src, dst) in enumerate(((k_hbm, kw), (v_hbm, vw)))
        ]

    def give_back(i, source, head):
        return [
            remote(
                src.at[i, head], dst.at[source * mine_count + i],
                ret_send.at[head, x, i], ret_recv.at[source, x, i], previous, head,
            )
            for x, (src, dst) in enumerate(((send_k, next_k), (send_v, next_v)))
        ]

    def across(i, source):
        theirs = (1 - source) * mine_count + i
        cols = block(theirs, d)
        return [
            remote(
                src, dst, chip_send.at[x, i], chip_recv.at[x, i], ctx, 1 - source
            )
            for x, (src, dst) in enumerate((
                (k_hbm.at[:, cols], kw.at[i, block(2 + source, rows)]),
                (v_hbm.at[:, cols], vw.at[i, block(2 + source, rows)]),
                (q_hbm.at[:, block(theirs, wide)], q_buf.at[i, source]),
                (g_hbm.at[:, block(theirs, wide)], g_buf.at[i, source]),
                (d_send.at[i], d_buf.at[i, source]),
                (dq_buf.at[i, 1 - source], dq_got.at[i]),
                (send_k.at[i, 2], part_k.at[i]),
                (send_v.at[i, 2], part_v.at[i]),
            ))
        ]

    barrier = pltpu.get_barrier_semaphore()

    def greet(where, head):
        pl.semaphore_signal(
            barrier, inc=1, device_id={"ctx": where, "head": head}, device_id_type=MESH
        )

    greet(ctx, other)
    for head in range(2):
        @pl.when(has_next)
        def _():
            greet(following, head)

        @pl.when(has_back)
        def _():
            greet(previous, head)

    for i in range(mine_count):
        for copy in load_mine(i):
            copy.start()
    for g in range(2 * mine_count):
        for copy in load_all(g):
            copy.start()

    pl.semaphore_wait(
        barrier, 1 + 2 * has_next.astype(jnp.int32) + 2 * has_back.astype(jnp.int32)
    )

    for i in range(mine_count):
        @pl.when(has_next)
        def _():
            for head in range(2):
                for copy in forward(i, me, head):
                    copy.start()

        for copy in across(i, me)[:4]:
            copy.start()

    @pl.when(jnp.logical_not(has_back))
    def _():
        zero = jnp.zeros((mine_count, 2 * rows, d), jnp.bfloat16)
        kw[:, : 2 * rows, :] = zero
        vw[:, : 2 * rows, :] = zero

    @pl.when(jnp.logical_not(has_next))
    def _():
        next_k[...] = jnp.zeros(next_k.shape, jnp.bfloat16)
        next_v[...] = jnp.zeros(next_v.shape, jnp.bfloat16)

    lane = lax.broadcasted_iota(jnp.int32, (rows, d), 1)

    def delta_of(g):
        for copy in load_all(g):
            copy.wait()
        total = jnp.zeros((rows, d), jnp.float32)
        for h in range(group):
            cols = slice(h * d, (h + 1) * d)
            product = g_all[g, :, cols].astype(jnp.float32) * o_all[g, :, cols].astype(jnp.float32)
            total = jnp.where(lane == h, jnp.sum(product, axis=1, keepdims=True), total)
        return total.astype(jnp.bfloat16)

    for i in range(mine_count):
        d_send[i] = delta_of(other * mine_count + i)
        across(i, me)[4].start()

    for token_block in range(2):
        first = (2 * ctx + token_block) * rows
        here_t = first + lax.broadcasted_iota(jnp.int32, (8, rows), 1)

        def document(index, state):
            end, start = state
            end = end + doc_ref[index]
            return end, jnp.where(end <= here_t, end, start)

        start = lax.fori_loop(
            0, doc_ref.shape[0], document,
            (jnp.int32(0), jnp.zeros((8, rows), jnp.int32)), unroll=8,
        )[1][:1]
        pos_u = first - 2 * rows + lax.broadcasted_iota(jnp.int32, (window, rows), 0)
        pos_t = first + lax.broadcasted_iota(jnp.int32, (window, rows), 1)
        allowed = (pos_u <= pos_t) & (pos_u >= start)
        bias[token_block] = jnp.where(allowed, 0.0, fill_value).astype(jnp.float32)

    for i in range(mine_count):
        d_buf[i, me] = delta_of(me * mine_count + i)

    minus = jnp.full((window, d), -1.0, jnp.bfloat16)
    factor = scale * math.log2(math.e)
    step = 2

    def unit(i, token_block):
        span = slice(token_block * rows, token_block * rows + window)
        k_all = kw[i, span]
        v_aug = jnp.concatenate([vw[i, span], minus], axis=1)

        for pair in range(group // step):
            heads = range(pair * step, (pair + 1) * step)
            q_rows = stack(q_buf, i, token_block, heads)
            deltas = d_buf[i, token_block]
            zero = jnp.zeros_like(deltas)
            d_rows = jnp.concatenate([jnp.where(lane == h, deltas, zero) for h in heads], axis=0)
            g_aug = jnp.concatenate([stack(g_buf, i, token_block, heads), d_rows], axis=1)
            scores = lax.dot_general(k_all, q_rows, NT, preferred_element_type=jnp.float32)
            scores = scores * factor + jnp.concatenate([bias[token_block]] * step, axis=1)
            top = jnp.max(scores, axis=0, keepdims=True)
            grown = jnp.exp2(scores - top)
            inverse = 1.0 / jnp.sum(grown, axis=0, keepdims=True)
            probs = grown * inverse
            cols = slice(pair * step * rows, (pair + 1) * step * rows)
            p_buf[i, token_block, :, cols] = probs.astype(jnp.bfloat16)
            diff = lax.dot_general(v_aug, g_aug, NT, preferred_element_type=jnp.float32)
            s_buf[i, token_block, :, cols] = (probs * diff).astype(jnp.bfloat16)

    def stack(ref, i, token_block, heads):
        return jnp.concatenate(
            [ref[i, token_block, :, h * d : (h + 1) * d] for h in heads], axis=0
        )

    def key_sum(buf, ref, i, token_block, low, high):
        return jnp.dot(
            buf[i, token_block, low:high], stack(ref, i, token_block, range(group)),
            preferred_element_type=jnp.float32,
        )

    def far_part(i, token_block):
        for buf, ref, send, carry, factor_out in (
            (s_buf, q_buf, send_k, acc_k, scale), (p_buf, g_buf, send_v, acc_v, None)
        ):
            total = key_sum(buf, ref, i, token_block, 0, (2 - token_block) * rows)
            if token_block == 0:
                carry[...] = total[rows:]
                total = total[:rows]
            else:
                total = total + carry[...]
            if factor_out is not None:
                total = total * factor_out
            send[i, token_block] = total.astype(jnp.bfloat16)

        @pl.when(has_back)
        def _():
            for copy in give_back(i, me, token_block):
                copy.start()

    def near_part(i):
        for buf, ref, send, own, near, factor_out in (
            (s_buf, q_buf, send_k, own_k, near_k, scale),
            (p_buf, g_buf, send_v, own_v, near_v, None),
        ):
            early = key_sum(buf, ref, i, 0, 2 * rows, 3 * rows)
            late = key_sum(buf, ref, i, 1, rows, 3 * rows)
            if factor_out is not None:
                early, late = early * factor_out, late * factor_out
            near[0] = early + late[:rows]
            near[1] = late[rows:]
            send[i, 2] = near[other].astype(jnp.bfloat16)
            own[i] = near[me]
        for copy in across(i, me)[6:]:
            copy.start()

    def query_part(i, token_block):
        span = slice(token_block * rows, token_block * rows + window)
        dq = lax.dot_general(
            kw[i, span], s_buf[i, token_block], TN, preferred_element_type=jnp.float32
        ) * scale
        for h in range(group):
            piece = dq[:, h * rows : (h + 1) * rows].T.astype(jnp.bfloat16)
            dq_buf[i, token_block, :, h * d : (h + 1) * d] = piece

        @pl.when(me != token_block)
        def _():
            across(i, me)[5].start()

    def one_group(i):
        for copy in load_mine(i):
            copy.wait()
        for copy in across(i, other)[:5]:
            copy.wait_recv()

        @pl.when(has_back)
        def _():
            for source in range(2):
                for copy in forward(i, source, me):
                    copy.wait_recv()

        for token_block in range(2):
            unit(i, token_block)
            far_part(i, token_block)

    for i in range(mine_count):
        one_group(i)
    for i in range(mine_count):
        near_part(i)
        for token_block in range(2):
            query_part(i, token_block)

    for i in range(mine_count):
        dq_out[:, block(me * mine_count + i, wide)] = dq_buf[i, me]
    for i in range(mine_count):
        for copy in across(i, other)[5:]:
            copy.wait_recv()
        dq_out[:, block(other * mine_count + i, wide)] = dq_got[i]

    for i in range(mine_count):
        @pl.when(has_next)
        def _():
            for source in range(2):
                for copy in give_back(i, source, me):
                    copy.wait_recv()

        for own, part, late, out in (
            (own_k, part_k, next_k, dk_out), (own_v, part_v, next_v, dv_out)
        ):
            g = me * mine_count + i
            total = own[i] + late[g].astype(jnp.float32)
            out[:, block(g, d)] = total.astype(jnp.bfloat16)
            g = other * mine_count + i
            total = part[i].astype(jnp.float32) + late[g].astype(jnp.float32)
            out[:, block(g, d)] = total.astype(jnp.bfloat16)

    for i in range(mine_count):
        for copy in across(i, me):
            copy.wait_send()

        @pl.when(has_next)
        def _():
            for head in range(2):
                for copy in forward(i, me, head):
                    copy.wait_send()

        @pl.when(has_back)
        def _():
            for head in range(2):
                for copy in give_back(i, me, head):
                    copy.wait_send()


def store_kernel(dq, dk, dv, dq_hbm, dk_hbm, dv_hbm, sem):
    copies = [
        pltpu.make_async_copy(src, dst, sem.at[x])
        for x, (src, dst) in enumerate(((dq, dq_hbm), (dk, dk_hbm), (dv, dv_hbm)))
    ]
    for copy in copies:
        copy.start()
    for copy in copies:
        copy.wait()


def on_device(n_ctx, n_head, queries, keys, values, attn_out, output_gradient, doc_lengths):
    d = HEAD_SIZE
    rows = queries.shape[0]
    kv_heads = keys.shape[1] // d
    group = queries.shape[1] // keys.shape[1]
    wide = group * d
    mine = kv_heads // n_head
    low, full = jnp.bfloat16, jnp.float32
    dma = pltpu.SemaphoreType.DMA
    any_space = pl.BlockSpec(memory_space=pl.ANY)
    results = pl.pallas_call(
        functools.partial(kernel, n_ctx, group, mine),
        out_shape=(
            pltpu.VMEM(queries.shape, low),
            pltpu.VMEM(keys.shape, low),
            pltpu.VMEM(values.shape, low),
        ),
        in_specs=[pl.BlockSpec(memory_space=pltpu.SMEM)] + [any_space] * 5,
        out_specs=(pl.BlockSpec(memory_space=pltpu.VMEM),) * 3,
        scratch_shapes=[
            pltpu.VMEM((mine, 2, rows, wide), low),
            pltpu.VMEM((mine, 2, rows, wide), low),
            pltpu.VMEM((kv_heads, rows, wide), low),
            pltpu.VMEM((kv_heads, rows, wide), low),
            pltpu.VMEM((mine, 2, rows, d), low),
            pltpu.VMEM((mine, rows, d), low),
            pltpu.VMEM((mine, 4 * rows, d), low),
            pltpu.VMEM((mine, 4 * rows, d), low),
            pltpu.VMEM((2, 3 * rows, rows), full),
            pltpu.VMEM((mine, 2, 3 * rows, group * rows), low),
            pltpu.VMEM((mine, 2, 3 * rows, group * rows), low),
            pltpu.VMEM((rows, d), full),
            pltpu.VMEM((rows, d), full),
            pltpu.VMEM((2, rows, d), full),
            pltpu.VMEM((2, rows, d), full),
            pltpu.VMEM((mine, rows, d), full),
            pltpu.VMEM((mine, rows, d), full),
            pltpu.VMEM((mine, 3, rows, d), low),
            pltpu.VMEM((mine, 3, rows, d), low),
            pltpu.VMEM((mine, rows, d), low),
            pltpu.VMEM((mine, rows, d), low),
            pltpu.VMEM((kv_heads, rows, d), low),
            pltpu.VMEM((kv_heads, rows, d), low),
            pltpu.VMEM((mine, 2, rows, wide), low),
            pltpu.VMEM((mine, rows, wide), low),
            dma((6, kv_heads)),
            dma((2, 2, mine)),
            dma((2, 2, mine)),
            dma((2, 2, mine)),
            dma((2, 2, mine)),
            dma((8, mine)),
            dma((8, mine)),
        ],
        compiler_params=pltpu.CompilerParams(collective_id=0, has_side_effects=True),
        name="packed_attention_backward",
    )(doc_lengths, queries, keys, values, attn_out, output_gradient)
    return pl.pallas_call(
        store_kernel,
        out_shape=tuple(jax.ShapeDtypeStruct(r.shape, low) for r in results),
        in_specs=[pl.BlockSpec(memory_space=pltpu.VMEM)] * 3,
        out_specs=(any_space,) * 3,
        scratch_shapes=[dma((3,))],
        name="store_gradients",
    )(*[pltpu.with_memory_space_constraint(r, pltpu.VMEM) for r in results])


def solution(mesh):
    n_ctx, n_head = mesh.shape["ctx"], mesh.shape["head"]
    rows = P(("ctx", "head"), None)
    return jax.shard_map(
        functools.partial(on_device, n_ctx, n_head),
        mesh=mesh,
        in_specs=(rows,) * 5 + (P(),),
        out_specs=(rows,) * 3,
        check_vma=False,
    )
```
